1024 devices in a mesh: section: 16 (over z), expert: 64 (over y, x, core).
Axes of the slice: x: 4, y: 8, z: 16, core: 2. Of those that a mesh axis runs over, the one named last changes fastest.
Arguments:
- next_grad: bfloat16 [16, 1024, 3584], P('section', 'expert'), may hold values from -6 to 6
- routes: int32 [16, 1024, 8], P('section', 'expert'), may hold values from 0 to 63, all different within a row; in each aligned block of 16 rows (0 to 15, 16 to 31, ..., all dimensions but the last counted through in order) at most 4 rows name the same one
- gates: float32 [16, 1024, 8], P('section', 'expert'), may hold values from 0.1 to 0.6
- saved: bfloat16 [16, 64, 256, 2048], P('section', 'expert'), may hold values from -5 to 5
- w_down: bfloat16 [64, 1024, 3584], P('expert'), may hold values from -0.1875 to 0.1875
Outputs:
- hidden_grads: bfloat16 [16, 64, 256, 2048], P('section', 'expert')
The draws below stay inside these ranges and needn't reach their ends.
Inputs may be any that keep to these rules, and one draw needn't show every extreme that they name: `routes`: each row names 8 different experts; among the 16 rows of one device no expert is named by more than 4 rows, and in every draw some expert is named by exactly 4 rows of some device.
All inputs are finite; a program needn't handle non-finite values.
Results may differ from the reference program's by a relative error of at most 0.005.
Values may be sent and summed in bfloat16 or wider, within the bound.
A program may use at most 32 MiB of HBM per device.

```python
import math
import jax
import jax.numpy as jnp
import numpy as np
from jax import lax

D = 3584
H = 1024
TOP = 8
TOK_DEV = 16
EXPERTS = 64
TOKENS = 1024
MOST = 4
SLOTS = 256
N_SECTION = 16
N_EXPERT = 64


def levels(own_key, dims, split, smallest, top_value):
    loudness, own = 1.0, jax.random.fold_in(own_key, 6)
    for dim, parts in split:
        heights = jnp.exp(jax.random.uniform(jax.random.fold_in(own, dim), (parts,), jnp.float32, smallest / len(split), top_value / len(split)))
        loudness = loudness * jnp.repeat(heights, dims[dim] // parts).reshape([-1 if axis == dim else 1 for axis in range(len(dims))])
    return loudness


def shared_out(own_key, own, number, rows, count, top, most, slope):
    ranking = jax.random.permutation(own_key, count)
    packed, common = shares(count, rows * top, most, slope, True), shares(count, rows * top, most, slope, False)
    places = jnp.arange(count)

    def named(sizes, rotation):
        used = int((sizes > 0).sum())
        fixed = max(1, used // 4)
        passed = fixed + (places - fixed + rotation * (used - fixed)) % max(1, count - fixed)
        return jnp.zeros((count,), jnp.int32).at[ranking[jnp.where(places < fixed, places, passed)]].set(jnp.asarray(sizes, jnp.int32))

    sizes = jnp.where(number % 4 == 0, named(packed, number // 4), named(common, number - number // 4 - 1))
    mixed = jax.random.permutation(jax.random.fold_in(own, 3), count)
    donor, taker = mixed[0:count // 2 * 2:2], mixed[1:count // 2 * 2:2]
    margin = jnp.minimum(sizes[donor] - 1, most - sizes[taker]) // 2
    margin = jnp.where((donor == ranking[0]) | (taker == ranking[0]) | (sizes[taker] == 0), 0, jnp.maximum(margin, 0))
    passed = jax.random.randint(jax.random.fold_in(own, 4), (count // 2,), 0, 1 << 20) % (margin + 1)
    sizes = sizes.at[donor].add(-passed).at[taker].add(passed)
    members = jnp.searchsorted(jnp.cumsum(sizes), jnp.arange(rows * top), side="right").astype(jnp.int32)
    grid = members.reshape(top, rows).T
    grid = grid[jax.random.permutation(jax.random.fold_in(own, 1), rows)]
    rotation = jax.random.randint(jax.random.fold_in(own, 2), (rows, 1), 0, top)
    return jnp.take_along_axis(grid, (jnp.arange(top)[None, :] + rotation) % top, axis=1)


def shares(count, total, most, skew, full):
    weights = [(1 << 20) // math.isqrt(standing ** skew) + 1 for standing in range(1, count + 1)]
    largest = most if full else min(most, max(-(-total // count), total * weights[0] // sum(weights)))
    least = 1 if total - largest >= count - 1 else 0
    holding, rest = [largest] + [least] * (count - 1), total - largest - least * (count - 1)
    while rest > 0:
        candidates = [i for i in range(1, count) if holding[i] < largest] or [i for i in range(1, count) if holding[i] < most]
        whole, budget = sum([weights[i] for i in candidates]), rest
        for i in candidates:
            extra = min(most - holding[i], max(1, budget * weights[i] // whole), rest)
            holding[i] = holding[i] + extra
            rest = rest - extra
    return np.array(holding)


def normal_values(stream_key, shape, width, bound, cuts=(), kind=jnp.bfloat16):
    result = jax.random.normal(stream_key, shape, jnp.float32) * width
    if len(cuts) > 0:
        result = levels(stream_key, shape, cuts, -0.22, 0.18) * result
    return jnp.clip(result, min=-bound, max=bound).astype(kind)


def setup_inputs(seed: int = 0) -> dict:
    key_list = jax.random.split(jax.random.key(seed), 6)
    next_grad = normal_values(key_list[0], (N_SECTION, TOKENS, D), 1.0, 6.0, ((0, 16), (1, 64)))
    routes_keys = jax.random.split(jax.random.fold_in(key_list[1], 1), N_SECTION * TOKENS // TOK_DEV)
    routes_turns = jax.random.permutation(jax.random.fold_in(key_list[1], 3), N_SECTION * TOKENS // TOK_DEV)
    routes = jax.vmap(lambda own, number: shared_out(jax.random.fold_in(key_list[1], 2), own, number, TOK_DEV, EXPERTS, TOP, MOST, 2))(routes_keys, routes_turns).reshape((N_SECTION, TOKENS, TOP))
    gates = jnp.clip(0.1 + 0.5 * jax.random.uniform(key_list[2], (N_SECTION, TOKENS, TOP), jnp.float32) ** levels(key_list[2], (N_SECTION, TOKENS, TOP), ((0, 16), (1, 64)), -0.2, 0.2), 0.1, 0.6)
    saved = normal_values(key_list[3], (N_SECTION, EXPERTS, SLOTS, 2 * H), 1.0, 5.0, ((0, 16), (1, 64)))
    w_down = normal_values(key_list[4], (EXPERTS, H, D), H ** -0.5, 0.1875, ((0, 64),))
    return {"next_grad": next_grad, "routes": routes, "gates": gates, "saved": saved, "w_down": w_down}


def one_section(args, w_down):
    grad, route, gate, saved_s = args
    expert_ids = jnp.arange(EXPERTS, dtype=jnp.int32)
    hit = jnp.sum((route[:, :, None] == expert_ids[None, None, :]).astype(jnp.int32), axis=1)
    blocks = hit.reshape(N_EXPERT, TOK_DEV, EXPERTS)
    before = (jnp.cumsum(blocks, axis=1) - blocks).reshape(TOKENS, EXPERTS).astype(jnp.int32)
    position = jnp.take_along_axis(before, route, axis=1).astype(jnp.int32)
    source = (jnp.arange(TOKENS, dtype=jnp.int32) // TOK_DEV)[:, None]
    slot = (source * MOST + position).astype(jnp.int32)
    rows = (gate[:, :, None] * grad[:, None, :].astype(jnp.float32)).astype(jnp.bfloat16)
    buffer = jnp.zeros((EXPERTS, SLOTS, D), jnp.bfloat16).at[route, slot].set(rows)

    def per_expert(pair):
        block, mat = pair
        return jnp.dot(block, mat.T, preferred_element_type=jnp.float32)

    hidden = lax.map(per_expert, (buffer, w_down))
    pre_gate = saved_s[..., :H].astype(jnp.float32)
    pre_up = saved_s[..., H:].astype(jnp.float32)
    sig = jax.nn.sigmoid(pre_gate)
    d_up = hidden * pre_gate * sig
    d_gate = hidden * pre_up * sig * (1.0 + pre_gate * (1.0 - sig))
    return jnp.concatenate([d_gate, d_up], axis=-1).astype(jnp.bfloat16)


def reference(next_grad, routes, gates, saved, w_down):
    incoming = jnp.roll(next_grad, -1, axis=0)
    return lax.map(lambda args: one_section(args, w_down), (incoming, routes, gates, saved))
```

```python
import functools

import jax
import jax.numpy as jnp
from jax import lax
from jax.experimental import pallas as pl
from jax.experimental.pallas import tpu as pltpu
from jax.sharding import PartitionSpec as P

MESH = pl.DeviceIdType.MESH
NX, NY, NCORE = 4, 8, 2
MOST = 4
CW = 512
BF, F32, I32 = jnp.bfloat16, jnp.float32, jnp.int32


def kernel(sections, nc, grad, routes, gates, saved, w_down, out,
           tok, row, snd, wv, sv, gfac, ufac, acc, rts, gts, meta, pick, weight, perm,
           s_y, r_y, s_x, r_x, s_z, r_z, s_r, r_r, l_in, l_w):
    s, e = lax.axis_index("section"), lax.axis_index("expert")
    y, x, c = e // (NX * NCORE), (e // NCORE) % NX, e % NCORE
    toks = grad.shape[0]
    width = w_down.shape[0]
    ncols = width // 4

    def at(ds, dy, dx, core):
        ss = (s + ds + sections) % sections
        yy, xx = (y + dy + NY) % NY, (x + dx + NX) % NX
        return (ss, (yy * NX + xx) * NCORE + core)

    in_copies = [
        pltpu.make_async_copy(routes, rts, l_in.at[0]),
        pltpu.make_async_copy(gates, gts, l_in.at[1]),
        pltpu.make_async_copy(saved, sv, l_in.at[2]),
    ]
    for cp in in_copies:
        cp.start()
    w_copies = [
        pltpu.make_async_copy(w_down.at[:, pl.ds(k * CW, CW)], wv.at[k], l_w.at[k]) for k in range(nc)
    ]
    for cp in w_copies:
        cp.start()

    barrier = pltpu.get_barrier_semaphore()
    peers = [at(0, 0, 0, 1 - c), at(0, 1, 0, c), at(0, -1, 0, c), at(1, 0, 0, c), at(-1, 0, 0, c)]
    peers += [at(0, 0, dx, core) for dx in (1, -1) for core in range(NCORE)]
    for peer in peers:
        pl.semaphore_signal(barrier, inc=1, device_id=peer, device_id_type=MESH)
    in_copies[0].wait()
    in_copies[1].wait()
    meta[0, y, :, 0:toks] = rts[...].astype(F32)
    meta[0, y, :, toks : 2 * toks] = gts[...]
    pl.semaphore_wait(barrier, len(peers))

    sends = []

    def send(src, dst, ssem, rsem, dev):
        cp = pltpu.make_async_remote_copy(
            src_ref=src, dst_ref=dst, send_sem=ssem, recv_sem=rsem, device_id=dev, device_id_type=MESH
        )
        cp.start()
        sends.append(cp)

    def recv(ref, ssem, rsem):
        pltpu.make_async_remote_copy(
            src_ref=ref, dst_ref=ref, send_sem=ssem, recv_sem=rsem, device_id=at(0, 1, 0, c), device_id_type=MESH
        ).wait_recv()

    def shard(k, b, yy):
        if k == nc:
            return meta.at[b, yy]
        return tok.at[k, pl.ds(pl.multiple_of((b * NY + yy) * toks, toks), toks), :]

    def far(b, up):
        return 4 if (b == 0) == up else 3

    def y_send(k, b, up, d):
        step = 1 if up else -1
        ref = shard(k, b, (y - step * d + NY) % NY)
        i = (b * 2 + int(up)) * 4 + d
        send(ref, ref, s_y.at[k, i], r_y.at[k, i], at(0, step, 0, c))

    def y_recv(k, b, up, d):
        step = 1 if up else -1
        i = (b * 2 + int(up)) * 4 + d - 1
        recv(shard(k, b, (y - step * d + NY) % NY), s_y.at[k, i], r_y.at[k, i])

    def first(k):
        if k < nc:
            recv(shard(k, 0, y), s_z.at[k], r_z.at[k])
        send(shard(k, 0, y), shard(k, 1, y), s_x.at[k], r_x.at[k], at(0, 0, 1, c))
        y_send(k, 0, True, 0)
        y_send(k, 0, False, 0)

    def first_b(k):
        recv(shard(k, 1, y), s_x.at[k], r_x.at[k])
        y_send(k, 1, True, 0)
        y_send(k, 1, False, 0)

    def hop(k, b, d):
        for up in (True, False):
            if d <= far(b, up):
                y_recv(k, b, up, d)
                if d < far(b, up):
                    y_send(k, b, up, d)

    targets = [
        [(x, c), (x, 1 - c), ((x - 1 + NX) % NX, 0), ((x - 1 + NX) % NX, 1)],
        [(x, c), (x, 1 - c), ((x + 1) % NX, 0), ((x + 1) % NX, 1)],
    ]

    def build_tables():
        lane = lax.broadcasted_iota(I32, (8, 128), 1)
        group = lane // toks
        tables = []
        for b in range(2):
            named = jnp.zeros((8, 128), F32)
            gate = jnp.zeros((8, 128), F32)
            for j in range(NY):
                m = meta[b, j]
                r = m if j == 0 else pltpu.roll(m, toks * j, 1)
                shift = (toks * j - toks) % 128
                g = m if shift == 0 else pltpu.roll(m, shift, 1)
                named = jnp.where(group == j, r, named)
                gate = jnp.where(group == j, g, gate)
            for xt, ct in targets[b]:
                expert = ((y * NX + xt) * NCORE + ct).astype(F32)
                tables.append(jnp.sum(jnp.where(named == expert, gate, 0.0), axis=0, keepdims=True))
        assign = jnp.concatenate(tables, axis=0)
        live = (assign > 0.0).astype(F32)
        a = lax.broadcasted_iota(I32, (128, 128), 0)
        b_ = lax.broadcasted_iota(I32, (128, 128), 1)
        tri = jnp.where((a // toks == b_ // toks) & (a < b_), 1.0, 0.0).astype(BF)
        before = jnp.dot(live.astype(BF), tri, preferred_element_type=F32)
        before = jnp.where(assign > 0.0, before, -1.0)
        ri = lax.broadcasted_iota(I32, (NY * MOST, 128), 0)
        li = lax.broadcasted_iota(I32, (NY * MOST, 128), 1)
        same = (ri // MOST) == (li // toks)
        place = (ri % MOST).astype(F32)
        for b in range(2):
            for t in range(4):
                i = b * 4 + t
                r0 = i * NY * MOST
                hit = same & (jnp.broadcast_to(before[i : i + 1], ri.shape) == place)
                wt = jnp.sum(jnp.where(hit, jnp.broadcast_to(assign[i : i + 1], ri.shape), 0.0), axis=1, keepdims=True)
                pick[r0 : r0 + NY * MOST, b * 128 : (b + 1) * 128] = jnp.where(hit, 1.0, 0.0).astype(BF)
                pick[r0 : r0 + NY * MOST, (1 - b) * 128 : (2 - b) * 128] = jnp.zeros((NY * MOST, 128), BF)
                weight[r0 : r0 + NY * MOST, :] = jnp.broadcast_to(wt, (NY * MOST, 128))

    def build_perm():
        slot = lax.broadcasted_iota(I32, (256, 256), 0)
        col = lax.broadcasted_iota(I32, (256, 256), 1)
        ys, xs, cs, p = slot // 32, (slot // 8) % NX, (slot // 4) % NCORE, slot % MOST
        dx = (xs - x + NX) % NX
        rel = jnp.where(dx == 0, 0, jnp.where(dx == 3, 1, jnp.where(dx == 1, 2, 3)))
        perm[...] = jnp.where(col == cs * 128 + rel * 32 + ys * 4 + p, 1.0, 0.0).astype(BF)

    def factors(q):
        n = sv.shape[0] // 4
        sl = slice(q * n, (q + 1) * n)
        pre_gate = sv[sl, :width].astype(F32)
        pre_up = sv[sl, width:].astype(F32)
        sig = jax.nn.sigmoid(pre_gate)
        ufac[sl, :] = pre_gate * sig
        gfac[sl, :] = pre_up * sig * (1.0 + pre_gate * (1.0 - sig))

    def select(k):
        n = NY * MOST
        res = jnp.dot(pick[...], tok[k], preferred_element_type=F32)
        wt = weight[...]
        rows = jnp.concatenate([res[:, i * 128 : (i + 1) * 128] * wt for i in range(CW // 128)], axis=1).astype(BF)
        for i, slot in ((1, 0), (5, 1), (2, 2), (3, 3), (6, 4), (7, 5)):
            snd[k, slot] = rows[i * n : (i + 1) * n]
        row[k, c, 0] = rows[0:n]
        row[k, c, 1] = rows[4 * n : 5 * n]
        for core in range(NCORE):
            send(snd.at[k, 2 + core], row.at[k, c, 2], s_r.at[k, 1 + core], r_r.at[k, 1 + c], at(0, 0, -1, core))
            send(snd.at[k, 4 + core], row.at[k, c, 3], s_r.at[k, 3 + core], r_r.at[k, 3 + c], at(0, 0, 1, core))
        send(snd.at[k, 0:2], row.at[k, c, 0:2], s_r.at[k, 0], r_r.at[k, 0], at(0, 0, 0, 1 - c))

    def main(k):
        recv(row.at[k, 1 - c, 0:2], s_r.at[k, 0], r_r.at[k, 0])
        for core in range(NCORE):
            recv(row.at[k, core, 2], s_r.at[k, 1 + core], r_r.at[k, 1 + core])
            recv(row.at[k, core, 3], s_r.at[k, 3 + core], r_r.at[k, 3 + core])
        w_copies[k].wait()
        lhs = jnp.dot(perm[...], row[k].reshape(256, CW), preferred_element_type=F32).astype(BF)
        for n in range(4):
            cols = slice(n * ncols, (n + 1) * ncols)
            part = lax.dot_general(lhs, wv[k, cols, :], (((1,), (1,)), ((), ())), preferred_element_type=F32)
            if k > 0:
                part = acc[:, cols] + part
            if k < nc - 1:
                acc[:, cols] = part
            else:
                ups = slice(width + n * ncols, width + (n + 1) * ncols)
                out[:, cols] = (part * gfac[:, cols]).astype(BF)
                out[:, ups] = (part * ufac[:, cols]).astype(BF)

    for k in range(nc):
        send(grad.at[:, pl.ds(k * CW, CW)], shard(k, 0, y), s_z.at[k], r_z.at[k], at(-1, 0, 0, c))

    order = [nc] + list(range(nc))

    def chunk(i):
        return order[i] if 0 <= i < len(order) else None

    for tick in range(len(order) + 6):
        todo = [
            (lambda k: first(k), 0),
            (lambda k: first_b(k), 1),
            (lambda k: hop(k, 0, 1), 1),
            (lambda k: hop(k, 1, 1), 2),
            (lambda k: hop(k, 0, 2), 2),
            (lambda k: hop(k, 1, 2), 3),
            (lambda k: hop(k, 0, 3), 3),
            (lambda k: hop(k, 1, 3), 4),
            (lambda k: hop(k, 0, 4), 4),
            (lambda k: hop(k, 1, 4), 5),
            (lambda k: build_tables() if k == nc else select(k), 5),
            (lambda k: None if k == nc else main(k), 6),
        ]
        for act, lag in todo:
            k = chunk(tick - lag)
            if k is not None:
                act(k)
        if tick == 0:
            build_perm()
            in_copies[2].wait()
        if tick < 4:
            factors(tick)

    for cp in sends:
        cp.wait_send()


def per_device(sections, next_grad, routes, gates, saved, w_down):
    toks, d = next_grad.shape[1:]
    slots, width2 = saved.shape[2:]
    width = width2 // 2
    nc = d // CW
    dma = pltpu.SemaphoreType.DMA
    res = pl.pallas_call(
        functools.partial(kernel, sections, nc),
        out_shape=jax.ShapeDtypeStruct((slots, width2), BF),
        in_specs=[pl.BlockSpec(memory_space=pltpu.HBM)] * 5,
        out_specs=pl.BlockSpec(memory_space=pltpu.VMEM),
        scratch_shapes=[
            pltpu.VMEM((nc, 2 * NY * toks, CW), BF),
            pltpu.VMEM((nc, NCORE, 4, NY * MOST, CW), BF),
            pltpu.VMEM((nc, 6, NY * MOST, CW), BF),
            pltpu.VMEM((nc, width, CW), BF),
            pltpu.VMEM((slots, width2), BF),
            pltpu.VMEM((slots, width), F32),
            pltpu.VMEM((slots, width), F32),
            pltpu.VMEM((slots, width), F32),
            pltpu.VMEM(routes.shape[:0:-1], I32),
            pltpu.VMEM(gates.shape[:0:-1], F32),
            pltpu.VMEM((2, NY, 8, 128), F32),
            pltpu.VMEM((256, 256), BF),
            pltpu.VMEM((256, 128), F32),
            pltpu.VMEM((256, 256), BF),
            dma((nc + 1, 16)),
            dma((nc + 1, 16)),
            dma((nc + 1,)),
            dma((nc + 1,)),
            dma((nc,)),
            dma((nc,)),
            dma((nc, 5)),
            dma((nc, 5)),
            dma((3,)),
            dma((nc,)),
        ],
        compiler_params=pltpu.CompilerParams(collective_id=0, has_side_effects=True, vmem_limit_bytes=40 << 20),
    )(*[pltpu.with_memory_space_constraint(v, pltpu.HBM) for v in (next_grad[0], routes[0].T, gates[0].T, saved[0, 0], w_down[0])])
    return res[None, None]


def solution(mesh):
    return jax.shard_map(
        functools.partial(per_device, mesh.shape["section"]),
        mesh=mesh,
        in_specs=(
            P("section", "expert", None),
            P("section", "expert", None),
            P("section", "expert", None),
            P("section", "expert", None, None),
            P("expert", None, None),
        ),
        out_specs=P("section", "expert", None, None),
        check_vma=False,
    )
```

```python
import functools

import jax
import jax.numpy as jnp
from jax import lax
from jax.experimental import pallas as pl
from jax.experimental.pallas import tpu as pltpu
from jax.sharding import PartitionSpec as P

MESH = pl.DeviceIdType.MESH
NX, NY, NCORE = 4, 8, 2
MOST = 4
CW = 512
BF, F32, I32 = jnp.bfloat16, jnp.float32, jnp.int32

ORDER = (
    (0, 0, 0, 0), (0, 0, 1, 0), (0, 1, 0, 0), (5, 7, 0, 2), (0, 1, 1, 0), (0, 2, 0, 0), (0, 2, 1, 0), (0, 3, 0, 0),
    (0, 3, 1, 0), (0, 4, 0, 0), (1, 0, 0, 1), (0, 4, 1, 0), (0, 5, 0, 0), (1, 0, 1, 1), (1, 1, 0, 1), (0, 5, 1, 0),
    (0, 6, 0, 0), (1, 1, 1, 1), (1, 2, 0, 1), (1, 2, 1, 1), (5, 7, 0, 3), (1, 3, 0, 1), (1, 3, 1, 1), (1, 4, 0, 1),
    (1, 0, 0, 2), (1, 4, 1, 1), (1, 5, 0, 1), (1, 0, 1, 2), (1, 1, 0, 2), (0, 6, 1, 0), (5, 7, 0, 4), (1, 5, 1, 1),
    (1, 1, 1, 2), (1, 2, 0, 2), (1, 2, 1, 2), (1, 3, 0, 2), (1, 3, 1, 2), (3, 7, 0, 0), (1, 0, 0, 3), (1, 4, 0, 2),
    (1, 4, 1, 2), (1, 6, 0, 1), (1, 0, 1, 3), (1, 5, 0, 2), (1, 1, 0, 3), (1, 6, 1, 1), (1, 5, 1, 2), (1, 1, 1, 3),
    (1, 2, 0, 3), (1, 2, 1, 3), (1, 3, 0, 3), (1, 3, 1, 3), (2, 0, 0, 0), (1, 4, 0, 3), (1, 4, 1, 3), (2, 0, 1, 0),
    (1, 6, 0, 2), (1, 5, 0, 3), (2, 1, 0, 0), (1, 6, 1, 2), (2, 1, 1, 0), (1, 5, 1, 3), (2, 2, 1, 0), (2, 2, 0, 0),
    (2, 3, 1, 0), (3, 0, 0, 0), (2, 3, 0, 0), (2, 4, 0, 0), (2, 4, 1, 0), (1, 6, 0, 3), (2, 5, 0, 0), (3, 1, 0, 0),
    (1, 6, 1, 3), (3, 2, 0, 0), (2, 5, 1, 0), (3, 3, 0, 0), (3, 4, 0, 0), (2, 6, 0, 0), (3, 5, 0, 0), (2, 6, 1, 0),
    (4, 0, 0, 0), (4, 1, 0, 0), (3, 6, 0, 0), (4, 2, 0, 0), (4, 3, 0, 0), (4, 4, 0, 0), (4, 5, 0, 0), (4, 6, 0, 0),
)


def kernel(sections, nc, grad, routes, gates, saved, w_down, out,
           tok, row, snd, wv, sv, gfac, ufac, acc, rts, gts, meta, pick, weight, perm,
           r_y, r_z, r_x, r_d, r_r, r_m, s_tok, l_in, l_w):
    s, e = lax.axis_index("section"), lax.axis_index("expert")
    y, x, c = e // (NX * NCORE), (e // NCORE) % NX, e % NCORE
    toks = grad.shape[0]
    width = w_down.shape[0]
    ncols = width // 4
    n = NY * MOST
    col = NY * toks

    def at(ds, dy, dx, core):
        ss = (s + ds + sections) % sections
        yy, xx = (y + dy + NY) % NY, (x + dx + NX) % NX
        return (ss, (yy * NX + xx) * NCORE + core)

    barrier = pltpu.get_barrier_semaphore()
    peers = [at(0, 0, 0, 1 - c), at(0, 1, 0, c), at(0, -1, 0, c), at(0, 0, 1, c), at(0, 0, -1, c)]
    peers += [at(1, 0, 0, c), at(-1, 0, 0, c), at(-1, 0, 1, c), at(1, 0, -1, c), at(0, 2, 0, c), at(0, -2, 0, c)]
    for peer in peers:
        pl.semaphore_signal(barrier, inc=1, device_id=peer, device_id_type=MESH)

    in_copies = [
        pltpu.make_async_copy(routes, rts, l_in.at[0]),
        pltpu.make_async_copy(gates, gts, l_in.at[1]),
        pltpu.make_async_copy(saved, sv, l_in.at[2]),
    ]
    for cp in in_copies:
        cp.start()
    w_copies = [
        pltpu.make_async_copy(w_down.at[:, pl.ds(k * CW, CW)], wv.at[pl.ds(k * width, width)], l_w.at[k])
        for k in range(nc)
    ]
    pl.semaphore_wait(barrier, len(peers))

    def send(src, dst, rsem, dev, k):
        pltpu.make_async_remote_copy(
            src_ref=src, dst_ref=dst, send_sem=s_tok.at[k], recv_sem=rsem,
            device_id=dev, device_id_type=MESH,
        ).start()

    def arrived(ref, rsem):
        pltpu.make_async_remote_copy(
            src_ref=ref, dst_ref=ref, send_sem=s_tok.at[0], recv_sem=rsem,
            device_id=at(0, 1, 0, c), device_id_type=MESH,
        ).wait_recv()

    def shard(k, b, yy):
        i = (c * 2 + b) * NY + yy
        return tok.at[k, pl.ds(pl.multiple_of(i * toks, toks), toks), :]

    def cols_of(k, core, b=None):
        m = NY if k == nc else col
        i = core * 2 if b is None else core * 2 + b
        rows = pl.ds(pl.multiple_of(i * m, m), m * (2 if b is None else 1))
        return meta.at[rows] if k == nc else tok.at[k, rows, :]

    def far(b, up):
        return 4 if (b == 0) == up else 3

    def y_send(k, b, up, d):
        step = 1 if up else -1
        ref = shard(k, b, (y - step * d + NY) % NY)
        send(ref, ref, r_y.at[k, b * 4 + d], at(0, step, 0, c), k)

    def y_arrived(k, b, d):
        arrived(tok.at[k, pl.ds(0, (2 if d < 4 else 1) * toks), :], r_y.at[k, b * 4 + d - 1])

    def first(k, b):
        arrived(shard(k, b, y), (r_z, r_x)[b].at[k])
        y_send(k, b, True, 0)
        y_send(k, b, False, 0)

    def hop(k, b, d):
        y_arrived(k, b, d)
        for up in (True, False):
            if d < far(b, up):
                y_send(k, b, up, d)

    def exchange(k, b):
        y_arrived(k, b, 4)
        ref = cols_of(k, c, b)
        send(ref, ref, r_d.at[k], at(0, 0, 0, 1 - c), k)

    def routing(step):
        def tile(dy):
            return meta.at[c * 2 * NY + (y + dy + NY) % NY]

        mine, before = cols_of(nc, c, 0), cols_of(nc, c, 1)
        if step == 1:
            for dy in (1, -1):
                send(tile(0), tile(0), r_m.at[0], at(0, dy, 0, c), nc)
        elif step == 2:
            arrived(meta.at[pl.ds(0, 2)], r_m.at[0])
            for dy, moved in ((3, (-1, 0, 1)), (-3, (-1, 0))):
                for j in moved:
                    send(tile(j), tile(j), r_m.at[1], at(0, dy, 0, c), nc)
        elif step == 3:
            arrived(meta.at[pl.ds(0, 5)], r_m.at[1])
            send(mine, before, r_m.at[2], at(0, 0, 1, c), nc)
            send(mine, mine, r_m.at[3], at(0, 0, 0, 1 - c), nc)
        else:
            arrived(before, r_m.at[2])
            send(before, before, r_m.at[3], at(0, 0, 0, 1 - c), nc)

    def build_tables():
        arrived(cols_of(nc, 1 - c), r_m.at[3])
        lane = lax.broadcasted_iota(I32, (8, 128), 1)
        group = lane // toks
        tables = []
        for cs in range(NCORE):
            for b in range(2):
                named = jnp.zeros((8, 128), F32)
                gate = jnp.zeros((8, 128), F32)
                for j in range(NY):
                    m = meta[(cs * 2 + b) * NY + j]
                    r = m if j == 0 else pltpu.roll(m, toks * j, 1)
                    shift = (toks * j - toks) % 128
                    g = m if shift == 0 else pltpu.roll(m, shift, 1)
                    named = jnp.where(group == j, r, named)
                    gate = jnp.where(group == j, g, gate)
                for xt in (x, (x - 1 + NX) % NX if b == 0 else (x + 1) % NX):
                    expert = ((y * NX + xt) * NCORE + c).astype(F32)
                    tables.append(jnp.sum(jnp.where(named == expert, gate, 0.0), axis=0, keepdims=True))
        assign = jnp.concatenate(tables, axis=0)
        live = jnp.where(assign > 0.0, 1.0, 0.0).astype(BF)
        from_ = lax.broadcasted_iota(I32, (128, 128), 0)
        to = lax.broadcasted_iota(I32, (128, 128), 1)
        tri = jnp.where((from_ // toks == to // toks) & (from_ < to), 1.0, 0.0).astype(BF)
        before = jnp.dot(live, tri, preferred_element_type=F32)
        before = jnp.where(assign > 0.0, before, -1.0)
        ri = lax.broadcasted_iota(I32, (n, 128), 0)
        li = lax.broadcasted_iota(I32, (n, 128), 1)
        same = (ri // MOST) == (li // toks)
        place = (ri % MOST).astype(F32)
        for cs in range(NCORE):
            for b in range(2):
                for t in range(2):
                    i = (cs * 2 + b) * 2 + t
                    r0 = (cs * 4 + t * 2 + b) * n
                    hit = same & (jnp.broadcast_to(before[i : i + 1], ri.shape) == place)
                    wt = jnp.where(hit, jnp.broadcast_to(assign[i : i + 1], ri.shape), 0.0)
                    pick[r0 : r0 + n, b * 128 : (b + 1) * 128] = jnp.where(hit, 1.0, 0.0).astype(BF)
                    pick[r0 : r0 + n, (1 - b) * 128 : (2 - b) * 128] = jnp.zeros((n, 128), BF)
                    weight[r0 : r0 + n, :] = jnp.broadcast_to(jnp.sum(wt, axis=1, keepdims=True), (n, 128))

    def build_perm():
        slot = lax.broadcasted_iota(I32, (256, 256), 0)
        place = lax.broadcasted_iota(I32, (256, 256), 1)
        ys, xs, cs, p = slot // 32, (slot // 8) % NX, (slot // 4) % NCORE, slot % MOST
        dx = (xs - x + NX) % NX
        rel = jnp.where(dx == 0, 0, jnp.where(dx == 3, 1, jnp.where(dx == 1, 2, 3)))
        perm[...] = jnp.where(place == rel * 64 + cs * 32 + ys * 4 + p, 1.0, 0.0).astype(BF)

    def factors(q):
        m = sv.shape[0] // 4
        sl = slice(q * m, (q + 1) * m)
        pre_gate = sv[sl, :width].astype(F32)
        pre_up = sv[sl, width:].astype(F32)
        sig = jax.nn.sigmoid(pre_gate)
        ufac[sl, :] = pre_gate * sig
        gfac[sl, :] = pre_up * sig * (1.0 + pre_gate * (1.0 - sig))

    def select(k):
        arrived(cols_of(k, 1 - c), r_d.at[k])
        for cs in range(NCORE):
            res = jnp.dot(pick[cs * 128 : (cs + 1) * 128, :], tok[k, cs * 2 * col : (cs + 1) * 2 * col, :],
                          preferred_element_type=F32)
            wt = weight[cs * 128 : (cs + 1) * 128, :]
            rows = jnp.concatenate([res[:, i * 128 : (i + 1) * 128] * wt for i in range(CW // 128)], axis=1).astype(BF)
            snd[k, 0, cs] = rows[2 * n : 3 * n]
            snd[k, 1, cs] = rows[3 * n : 4 * n]
            row[k, 0, cs] = rows[0:n]
            row[k, 1, cs] = rows[n : 2 * n]
        send(snd.at[k, 0], row.at[k, 2], r_r.at[k], at(0, 0, -1, c), k)
        send(snd.at[k, 1], row.at[k, 3], r_r.at[k], at(0, 0, 1, c), k)

    def main(k):
        arrived(row.at[k, 2:4], r_r.at[k])
        w_copies[k].wait()
        lhs = jnp.dot(perm[...], row[k].reshape(256, CW), preferred_element_type=F32).astype(BF)
        for i in range(4):
            cols = slice(i * ncols, (i + 1) * ncols)
            wk = wv[k * width + i * ncols : k * width + (i + 1) * ncols, :]
            part = lax.dot_general(lhs, wk, (((1,), (1,)), ((), ())), preferred_element_type=F32)
            if k > 0:
                part = acc[:, cols] + part
            if k < nc - 1:
                acc[:, cols] = part
            else:
                out[:, cols] = (part * gfac[:, cols]).astype(BF)
                out[:, width + i * ncols : width + (i + 1) * ncols] = (part * ufac[:, cols]).astype(BF)

    for k in range(nc):
        part = grad.at[:, pl.ds(k * CW, CW)]
        send(part, shard(k, 0, y), r_z.at[k], at(-1, 0, 0, c), k)
        send(part, shard(k, 1, y), r_x.at[k], at(-1, 0, 1, c), k)
    for cp in w_copies:
        cp.start()
    in_copies[0].wait()
    in_copies[1].wait()
    own = (c * 2) * NY + y
    meta[own, :, 0:toks] = rts[...].astype(F32)
    meta[own, :, toks : 2 * toks] = gts[...]
    routing(1)
    build_perm()
    in_copies[2].wait()
    for q in range(4):
        factors(q)

    for kind, k, b, d in ORDER:
        with jax.named_scope(f"{'fhesmq'[kind]}{b}{d}_{k}"):
            if kind == 0:
                first(k, b)
            elif kind == 1:
                hop(k, b, d)
            elif kind == 2:
                exchange(k, b)
            elif kind == 3:
                build_tables() if k == nc else select(k)
            elif kind == 4:
                main(k)
            else:
                routing(d)

    for k in range(nc):
        ref = wv.at[pl.ds(0, 16 * toks + 2 * col + 4 * n)]
        pltpu.make_async_copy(ref, ref, s_tok.at[k]).wait()
    ref = meta.at[pl.ds(0, 15 + 2 * NY)]
    pltpu.make_async_copy(ref, ref, s_tok.at[nc]).wait()


def per_device(sections, next_grad, routes, gates, saved, w_down):
    toks, d = next_grad.shape[1:]
    slots, width2 = saved.shape[2:]
    width = width2 // 2
    nc = d // CW
    dma = pltpu.SemaphoreType.DMA
    args = (next_grad[0], routes[0].T, gates[0].T, saved[0, 0], w_down[0])
    res = pl.pallas_call(
        functools.partial(kernel, sections, nc),
        out_shape=jax.ShapeDtypeStruct((slots, width2), BF),
        in_specs=[pl.BlockSpec(memory_space=pltpu.HBM)] * 5,
        out_specs=pl.BlockSpec(memory_space=pltpu.VMEM),
        scratch_shapes=[
            pltpu.VMEM((nc, NCORE * 2 * NY * toks, CW), BF),
            pltpu.VMEM((nc, 4, NCORE, NY * MOST, CW), BF),
            pltpu.VMEM((nc, 2, NCORE, NY * MOST, CW), BF),
            pltpu.VMEM((nc * width, CW), BF),
            pltpu.VMEM((slots, width2), BF),
            pltpu.VMEM((slots, width), F32),
            pltpu.VMEM((slots, width), F32),
            pltpu.VMEM((slots, width), F32),
            pltpu.VMEM(routes.shape[:0:-1], I32),
            pltpu.VMEM(gates.shape[:0:-1], F32),
            pltpu.VMEM((NCORE * 2 * NY, 8, 128), F32),
            pltpu.VMEM((256, 256), BF),
            pltpu.VMEM((256, 128), F32),
            pltpu.VMEM((256, 256), BF),
            dma((nc, 8)),
            dma((nc,)),
            dma((nc,)),
            dma((nc,)),
            dma((nc,)),
            dma((4,)),
            dma((nc + 1,)),
            dma((3,)),
            dma((nc,)),
        ],
        compiler_params=pltpu.CompilerParams(collective_id=0, has_side_effects=True, vmem_limit_bytes=40 << 20),
    )(*[pltpu.with_memory_space_constraint(v, pltpu.HBM) for v in args])
    return res[None, None]


def solution(mesh):
    return jax.shard_map(
        functools.partial(per_device, mesh.shape["section"]),
        mesh=mesh,
        in_specs=(
            P("section", "expert", None),
            P("section", "expert", None),
            P("section", "expert", None),
            P("section", "expert", None, None),
            P("expert", None, None),
        ),
        out_specs=P("section", "expert", None, None),
        check_vma=False,
    )
```

```python
import functools

import jax
import jax.numpy as jnp
from jax import lax
from jax.experimental import pallas as pl
from jax.experimental.pallas import tpu as pltpu
from jax.sharding import PartitionSpec as P

MESH = pl.DeviceIdType.MESH
NX, NY, NCORE = 4, 8, 2
MOST = 4
CW = 512
BF, F32, I32 = jnp.bfloat16, jnp.float32, jnp.int32

ORDER = (
    (0, 0, 0, 0), (0, 0, 1, 0), (5, 7, 0, 2), (0, 1, 0, 0), (0, 1, 1, 0), (0, 2, 0, 0), (0, 2, 1, 0), (0, 3, 0, 0),
    (0, 3, 1, 0), (0, 4, 0, 0), (1, 0, 0, 1), (0, 4, 1, 0), (0, 5, 0, 0), (1, 0, 1, 1), (0, 5, 1, 0), (0, 6, 0, 0),
    (1, 1, 0, 1), (0, 6, 1, 0), (1, 1, 1, 1), (1, 2, 0, 1), (5, 7, 0, 3), (1, 2, 1, 1), (1, 3, 0, 1), (1, 3, 1, 1),
    (1, 4, 0, 1), (1, 0, 0, 2), (2, 0, 0, 0), (1, 4, 1, 1), (1, 5, 0, 1), (1, 0, 1, 2), (2, 0, 1, 0), (1, 5, 1, 1),
    (1, 6, 0, 1), (1, 1, 0, 2), (5, 7, 0, 4), (2, 1, 0, 0), (1, 6, 1, 1), (1, 1, 1, 2), (2, 1, 1, 0), (1, 2, 0, 2),
    (3, 7, 0, 0), (3, 0, 0, 0), (3, 1, 0, 0), (2, 2, 0, 0), (1, 2, 1, 2), (2, 2, 1, 0), (1, 3, 0, 2), (2, 3, 0, 0),
    (1, 3, 1, 2), (2, 3, 1, 0), (1, 4, 0, 2), (2, 4, 0, 0), (1, 0, 0, 3), (1, 4, 1, 2), (3, 2, 0, 0), (3, 3, 0, 0),
    (2, 4, 1, 0), (1, 0, 1, 3), (1, 5, 0, 2), (2, 5, 0, 0), (1, 5, 1, 2), (2, 5, 1, 0), (1, 6, 0, 2), (3, 4, 0, 0),
    (3, 5, 0, 0), (1, 1, 0, 3), (1, 1, 1, 3), (2, 6, 0, 0), (1, 6, 1, 2), (2, 6, 1, 0), (1, 2, 0, 3), (1, 2, 1, 3),
    (1, 3, 0, 3), (3, 6, 0, 0), (1, 3, 1, 3), (1, 4, 0, 3), (2, 0, 0, 1), (2, 0, 1, 1), (1, 4, 1, 3), (1, 5, 0, 3),
    (1, 5, 1, 3), (3, 0, 0, 1), (2, 1, 0, 1), (2, 1, 1, 1), (1, 6, 0, 3), (1, 6, 1, 3), (2, 2, 1, 1), (2, 2, 0, 1),
    (2, 3, 1, 1), (3, 1, 0, 1), (2, 3, 0, 1), (2, 4, 0, 1), (3, 2, 0, 1), (2, 4, 1, 1), (2, 5, 0, 1), (3, 3, 0, 1),
    (2, 5, 1, 1), (3, 4, 0, 1), (2, 6, 0, 1), (2, 6, 1, 1), (3, 5, 0, 1), (4, 0, 0, 0), (3, 6, 0, 1), (4, 1, 0, 0),
    (4, 2, 0, 0), (4, 3, 0, 0), (4, 4, 0, 0), (4, 5, 0, 0), (4, 6, 0, 0),
)


def kernel(sections, nc, grad, routes, gates, saved, w_down, out,
           tok, row, snd, wv, sv, gfac, ufac, acc, rts, gts, meta, pick, weight, perm,
           r_y, r_z, r_x, r_d, r_r, r_m, s_tok, l_in, l_w):
    s, e = lax.axis_index("section"), lax.axis_index("expert")
    y, x, c = e // (NX * NCORE), (e // NCORE) % NX, e % NCORE
    toks = grad.shape[0]
    width = w_down.shape[0]
    ncols = width // 4
    n = NY * MOST
    half = NY * toks // 2
    m16 = n // 2

    def at(ds, dy, dx, core):
        ss = (s + ds + sections) % sections
        yy, xx = (y + dy + NY) % NY, (x + dx + NX) % NX
        return (ss, (yy * NX + xx) * NCORE + core)

    barrier = pltpu.get_barrier_semaphore()
    peers = [at(0, 0, 0, 1 - c), at(0, 1, 0, c), at(0, -1, 0, c), at(0, 0, 1, c), at(0, 0, -1, c)]
    peers += [at(1, 0, 0, c), at(-1, 0, 0, c), at(-1, 0, 1, c), at(1, 0, -1, c), at(0, 2, 0, c), at(0, -2, 0, c)]
    for peer in peers:
        pl.semaphore_signal(barrier, inc=1, device_id=peer, device_id_type=MESH)

    in_copies = [
        pltpu.make_async_copy(routes, rts, l_in.at[0]),
        pltpu.make_async_copy(gates, gts, l_in.at[1]),
        pltpu.make_async_copy(saved, sv, l_in.at[2]),
    ]
    for cp in in_copies:
        cp.start()
    w_copies = [
        pltpu.make_async_copy(w_down.at[:, pl.ds(k * CW, CW)], wv.at[pl.ds(k * width, width)], l_w.at[k])
        for k in range(nc)
    ]
    pl.semaphore_wait(barrier, len(peers))

    def send(src, dst, rsem, dev, k):
        pltpu.make_async_remote_copy(
            src_ref=src, dst_ref=dst, send_sem=s_tok.at[k], recv_sem=rsem,
            device_id=dev, device_id_type=MESH,
        ).start()

    def arrived(ref, rsem):
        pltpu.make_async_remote_copy(
            src_ref=ref, dst_ref=ref, send_sem=s_tok.at[0], recv_sem=rsem,
            device_id=at(0, 1, 0, c), device_id_type=MESH,
        ).wait_recv()

    def shard(k, b, dy):
        j = (dy + 2) % NY
        rows = pl.multiple_of((c * 2 + b) * half + (j % (NY // 2)) * toks, toks)
        return tok.at[k, j // (NY // 2), pl.ds(rows, toks), :]

    def far(b, up):
        return 4 if (b == 0) == up else 3

    def y_send(k, b, up, d):
        step = 1 if up else -1
        send(shard(k, b, -step * d), shard(k, b, -step * (d + 1)), r_y.at[k, b * 4 + d], at(0, step, 0, c), k)

    def y_arrived(k, b, d):
        arrived(tok.at[k, 0, pl.ds(0, (2 if d < 4 else 1) * toks), :], r_y.at[k, b * 4 + d - 1])

    def first(k, b):
        arrived(shard(k, b, 0), (r_z, r_x)[b].at[k])
        y_send(k, b, True, 0)
        y_send(k, b, False, 0)

    def hop(k, b, d):
        y_arrived(k, b, d)
        for up in (True, False):
            if d < far(b, up):
                y_send(k, b, up, d)

    def exchange(k, b, p):
        if p == 1:
            y_arrived(k, b, 4)
        ref = tok.at[k, p, pl.ds(pl.multiple_of((c * 2 + b) * half, half), half), :]
        send(ref, ref, r_d.at[k, p], at(0, 0, 0, 1 - c), k)

    def routing(step):
        def tile(dy):
            return meta.at[c * 2 * NY + (y + dy + NY) % NY]

        mine, before = [meta.at[pl.ds(pl.multiple_of((c * 2 + b) * NY, NY), NY)] for b in range(2)]
        if step == 1:
            for dy in (1, -1):
                send(tile(0), tile(0), r_m.at[0], at(0, dy, 0, c), nc)
        elif step == 2:
            arrived(meta.at[pl.ds(0, 2)], r_m.at[0])
            for dy, moved in ((3, (-1, 0, 1)), (-3, (-1, 0))):
                for j in moved:
                    send(tile(j), tile(j), r_m.at[1], at(0, dy, 0, c), nc)
        elif step == 3:
            arrived(meta.at[pl.ds(0, 5)], r_m.at[1])
            send(mine, before, r_m.at[2], at(0, 0, 1, c), nc)
            send(mine, mine, r_m.at[3], at(0, 0, 0, 1 - c), nc)
        else:
            arrived(before, r_m.at[2])
            send(before, before, r_m.at[3], at(0, 0, 0, 1 - c), nc)

    def build_tables():
        arrived(meta.at[pl.ds(0, 2 * NY)], r_m.at[3])
        lane = lax.broadcasted_iota(I32, (8, 128), 1)
        group = lane // toks
        tables = []
        for cs in range(NCORE):
            for b in range(2):
                named = jnp.zeros((8, 128), F32)
                gate = jnp.zeros((8, 128), F32)
                for j in range(NY):
                    m = meta[(cs * 2 + b) * NY + (y + j - 2 + NY) % NY]
                    r = m if j == 0 else pltpu.roll(m, toks * j, 1)
                    shift = (toks * j - toks) % 128
                    g = m if shift == 0 else pltpu.roll(m, shift, 1)
                    named = jnp.where(group == j, r, named)
                    gate = jnp.where(group == j, g, gate)
                for xt in (x, (x - 1 + NX) % NX if b == 0 else (x + 1) % NX):
                    expert = ((y * NX + xt) * NCORE + c).astype(F32)
                    tables.append(jnp.sum(jnp.where(named == expert, gate, 0.0), axis=0, keepdims=True))
        assign = jnp.concatenate(tables, axis=0)
        live = jnp.where(assign > 0.0, 1.0, 0.0).astype(BF)
        from_ = lax.broadcasted_iota(I32, (128, 128), 0)
        to = lax.broadcasted_iota(I32, (128, 128), 1)
        tri = jnp.where((from_ // toks == to // toks) & (from_ < to), 1.0, 0.0).astype(BF)
        before = jnp.dot(live, tri, preferred_element_type=F32)
        before = jnp.where(assign > 0.0, before, -1.0)
        turned = [(assign, before), (pltpu.roll(assign, half, 1), pltpu.roll(before, half, 1))]
        ri = lax.broadcasted_iota(I32, (m16, 128), 0)
        li = lax.broadcasted_iota(I32, (m16, 128), 1)
        same = (ri // MOST) == (li % half) // toks
        place = (ri % MOST).astype(F32)
        for p in range(2):
            for cs in range(NCORE):
                for b in range(2):
                    gates_, places_ = turned[0 if b == p else 1]
                    here = same & (li // half == b)
                    for t in range(2):
                        i = (cs * 2 + b) * 2 + t
                        r0 = (t * 4 + b * 2 + cs) * m16
                        hit = here & (jnp.broadcast_to(places_[i : i + 1], ri.shape) == place)
                        wt = jnp.where(hit, jnp.broadcast_to(gates_[i : i + 1], ri.shape), 0.0)
                        rows = slice(r0, r0 + m16)
                        pick[p, rows, cs * 128 : (cs + 1) * 128] = jnp.where(hit, 1.0, 0.0).astype(BF)
                        pick[p, rows, (1 - cs) * 128 : (2 - cs) * 128] = jnp.zeros((m16, 128), BF)
                        weight[p, rows, :] = jnp.broadcast_to(jnp.sum(wt, axis=1, keepdims=True), (m16, 128))

    def build_perm():
        slot = lax.broadcasted_iota(I32, (256, 256), 0)
        place = lax.broadcasted_iota(I32, (256, 256), 1)
        ys, xs, cs, p = slot // 32, (slot // 8) % NX, (slot // 4) % NCORE, slot % MOST
        dx = (xs - x + NX) % NX
        rel = jnp.where(dx == 0, 0, jnp.where(dx == 3, 1, jnp.where(dx == 1, 2, 3)))
        j = (ys - y + 2 + NY) % NY
        spot = (j // 4) * 128 + rel * 32 + cs * 16 + (j % 4) * MOST + p
        perm[...] = jnp.where(place == spot, 1.0, 0.0).astype(BF)

    def factors(q):
        m = sv.shape[0] // 4
        sl = slice(q * m, (q + 1) * m)
        pre_gate = sv[sl, :width].astype(F32)
        pre_up = sv[sl, width:].astype(F32)
        sig = jax.nn.sigmoid(pre_gate)
        ufac[sl, :] = pre_gate * sig
        gfac[sl, :] = pre_up * sig * (1.0 + pre_gate * (1.0 - sig))

    def select(k, p):
        arrived(tok.at[k, p, pl.ds(0, 2 * half), :], r_d.at[k, p])
        res = jnp.dot(pick[p], tok[k, p], preferred_element_type=F32)
        wt = weight[p]
        rows = jnp.concatenate([res[:, i * 128 : (i + 1) * 128] * wt for i in range(CW // 128)], axis=1).astype(BF)
        snd[k, p, 0] = rows[2 * n : 3 * n]
        snd[k, p, 1] = rows[3 * n : 4 * n]
        row[k, p, 0] = rows[0:n]
        row[k, p, 1] = rows[n : 2 * n]
        send(snd.at[k, p, 0], row.at[k, p, 2], r_r.at[k], at(0, 0, -1, c), k)
        send(snd.at[k, p, 1], row.at[k, p, 3], r_r.at[k], at(0, 0, 1, c), k)

    def main(k):
        arrived(wv.at[pl.ds(0, 4 * n)], r_r.at[k])
        w_copies[k].wait()
        lhs = jnp.dot(perm[...], row[k].reshape(256, CW), preferred_element_type=F32).astype(BF)
        for i in range(4):
            cols = slice(i * ncols, (i + 1) * ncols)
            wk = wv[k * width + i * ncols : k * width + (i + 1) * ncols, :]
            part = lax.dot_general(lhs, wk, (((1,), (1,)), ((), ())), preferred_element_type=F32)
            if k > 0:
                part = acc[:, cols] + part
            if k < nc - 1:
                acc[:, cols] = part
            else:
                out[:, cols] = (part * gfac[:, cols]).astype(BF)
                out[:, width + i * ncols : width + (i + 1) * ncols] = (part * ufac[:, cols]).astype(BF)

    for k in range(nc):
        part = grad.at[:, pl.ds(k * CW, CW)]
        send(part, shard(k, 0, 0), r_z.at[k], at(-1, 0, 0, c), k)
        send(part, shard(k, 1, 0), r_x.at[k], at(-1, 0, 1, c), k)
    for cp in w_copies:
        cp.start()
    in_copies[0].wait()
    in_copies[1].wait()
    own = (c * 2) * NY + y
    meta[own, :, 0:toks] = rts[...].astype(F32)
    meta[own, :, toks : 2 * toks] = gts[...]
    routing(1)
    build_perm()
    in_copies[2].wait()
    for q in range(4):
        factors(q)

    for kind, k, b, d in ORDER:
        with jax.named_scope(f"{'fhesmq'[kind]}{b}{d}_{k}"):
            if kind == 0:
                first(k, b)
            elif kind == 1:
                hop(k, b, d)
            elif kind == 2:
                exchange(k, b, d)
            elif kind == 3:
                build_tables() if k == nc else select(k, d)
            elif kind == 4:
                main(k)
            else:
                routing(d)

    for k in range(nc):
        ref = wv.at[pl.ds(0, 16 * toks + 4 * half + 4 * n)]
        pltpu.make_async_copy(ref, ref, s_tok.at[k]).wait()
    ref = meta.at[pl.ds(0, 15 + 2 * NY)]
    pltpu.make_async_copy(ref, ref, s_tok.at[nc]).wait()


def per_device(sections, next_grad, routes, gates, saved, w_down):
    toks, d = next_grad.shape[1:]
    slots, width2 = saved.shape[2:]
    width = width2 // 2
    nc = d // CW
    dma = pltpu.SemaphoreType.DMA
    args = (next_grad[0], routes[0].T, gates[0].T, saved[0, 0], w_down[0])
    res = pl.pallas_call(
        functools.partial(kernel, sections, nc),
        out_shape=jax.ShapeDtypeStruct((slots, width2), BF),
        in_specs=[pl.BlockSpec(memory_space=pltpu.HBM)] * 5,
        out_specs=pl.BlockSpec(memory_space=pltpu.VMEM),
        scratch_shapes=[
            pltpu.VMEM((nc, 2, NCORE * NY * toks, CW), BF),
            pltpu.VMEM((nc, 2, 4, NY * MOST, CW), BF),
            pltpu.VMEM((nc, 2, 2, NY * MOST, CW), BF),
            pltpu.VMEM((nc * width, CW), BF),
            pltpu.VMEM((slots, width2), BF),
            pltpu.VMEM((slots, width), F32),
            pltpu.VMEM((slots, width), F32),
            pltpu.VMEM((slots, width), F32),
            pltpu.VMEM(routes.shape[:0:-1], I32),
            pltpu.VMEM(gates.shape[:0:-1], F32),
            pltpu.VMEM((NCORE * 2 * NY, 8, 128), F32),
            pltpu.VMEM((2, 128, 256), BF),
            pltpu.VMEM((2, 128, 128), F32),
            pltpu.VMEM((256, 256), BF),
            dma((nc, 8)),
            dma((nc,)),
            dma((nc,)),
            dma((nc, 2)),
            dma((nc,)),
            dma((4,)),
            dma((nc + 1,)),
            dma((3,)),
            dma((nc,)),
        ],
        compiler_params=pltpu.CompilerParams(collective_id=0, has_side_effects=True, vmem_limit_bytes=40 << 20),
    )(*[pltpu.with_memory_space_constraint(v, pltpu.HBM) for v in args])
    return res[None, None]


def solution(mesh):
    return jax.shard_map(
        functools.partial(per_device, mesh.shape["section"]),
        mesh=mesh,
        in_specs=(
            P("section", "expert", None),
            P("section", "expert", None),
            P("section", "expert", None),
            P("section", "expert", None, None),
            P("expert", None, None),
        ),
        out_specs=P("section", "expert", None, None),
        check_vma=False,
    )
```

```python
import functools

import jax
import jax.numpy as jnp
from jax import lax
from jax.experimental import pallas as pl
from jax.experimental.pallas import tpu as pltpu
from jax.sharding import PartitionSpec as P

MESH = pl.DeviceIdType.MESH
NX, NY, NCORE = 4, 8, 2
MOST = 4
CW = 512
BF, F32, I32 = jnp.bfloat16, jnp.float32, jnp.int32

ORDER = (
    (0, 0, 0, 0), (0, 0, 1, 0), (5, 7, 0, 2), (0, 1, 0, 0), (0, 1, 1, 0), (0, 2, 0, 0), (0, 2, 1, 0), (0, 3, 0, 0),
    (0, 3, 1, 0), (0, 4, 0, 0), (1, 0, 0, 1), (0, 4, 1, 0), (0, 5, 0, 0), (1, 0, 1, 1), (0, 5, 1, 0), (0, 6, 0, 0),
    (1, 1, 0, 1), (0, 6, 1, 0), (1, 1, 1, 1), (1, 2, 0, 1), (5, 7, 0, 3), (1, 2, 1, 1), (1, 3, 0, 1), (1, 3, 1, 1),
    (1, 4, 0, 1), (1, 0, 0, 2), (2, 0, 0, 0), (1, 4, 1, 1), (1, 5, 0, 1), (1, 0, 1, 2), (2, 0, 1, 0), (1, 5, 1, 1),
    (1, 6, 0, 1), (1, 1, 0, 2), (5, 7, 0, 4), (2, 1, 0, 0), (1, 6, 1, 1), (1, 1, 1, 2), (2, 1, 1, 0), (1, 2, 0, 2),
    (3, 7, 0, 0), (3, 0, 0, 0), (3, 1, 0, 0), (2, 2, 0, 0), (1, 2, 1, 2), (2, 2, 1, 0), (1, 3, 0, 2), (2, 3, 0, 0),
    (1, 3, 1, 2), (2, 3, 1, 0), (1, 4, 0, 2), (2, 4, 0, 0), (1, 0, 0, 3), (1, 4, 1, 2), (3, 2, 0, 0), (3, 3, 0, 0),
    (2, 4, 1, 0), (1, 0, 1, 3), (1, 5, 0, 2), (2, 5, 0, 0), (1, 5, 1, 2), (2, 5, 1, 0), (1, 6, 0, 2), (3, 4, 0, 0),
    (3, 5, 0, 0), (1, 1, 0, 3), (1, 1, 1, 3), (2, 6, 0, 0), (1, 6, 1, 2), (2, 6, 1, 0), (1, 2, 0, 3), (1, 2, 1, 3),
    (1, 3, 0, 3), (3, 6, 0, 0), (1, 3, 1, 3), (1, 4, 0, 3), (2, 0, 0, 1), (2, 0, 1, 1), (1, 4, 1, 3), (1, 5, 0, 3),
    (1, 5, 1, 3), (3, 0, 0, 1), (2, 1, 0, 1), (2, 1, 1, 1), (1, 6, 0, 3), (1, 6, 1, 3), (2, 2, 1, 1), (2, 2, 0, 1),
    (2, 3, 1, 1), (3, 1, 0, 1), (2, 3, 0, 1), (2, 4, 0, 1), (3, 2, 0, 1), (2, 4, 1, 1), (2, 5, 0, 1), (3, 3, 0, 1),
    (2, 5, 1, 1), (3, 4, 0, 1), (2, 6, 0, 1), (2, 6, 1, 1), (3, 5, 0, 1), (4, 0, 0, 0), (3, 6, 0, 1), (4, 1, 0, 0),
    (4, 2, 0, 0), (4, 3, 0, 0), (4, 4, 0, 0), (4, 5, 0, 0), (4, 6, 0, 0),
)


def kernel(sections, nc, grad, routes, gates, saved, w_down, out,
           tok, row, snd, wv, sv, gfac, ufac, acc, rts, gts, meta, pick, weight, perm,
           r_y, r_z, r_x, r_d, r_r, r_m, s_tok, l_in, l_w):
    s, e = lax.axis_index("section"), lax.axis_index("expert")
    y, x, c = e // (NX * NCORE), (e // NCORE) % NX, e % NCORE
    toks = grad.shape[0]
    width = w_down.shape[0]
    ncols = width // 4
    n = NY * MOST
    half = NY * toks // 2
    m16 = n // 2

    def at(ds, dy, dx, core):
        ss = (s + ds + sections) % sections
        yy, xx = (y + dy + NY) % NY, (x + dx + NX) % NX
        return (ss, (yy * NX + xx) * NCORE + core)

    barrier = pltpu.get_barrier_semaphore()
    peers = [at(0, 0, 0, 1 - c), at(0, 1, 0, c), at(0, -1, 0, c), at(0, 0, 1, c), at(0, 0, -1, c)]
    peers += [at(1, 0, 0, c), at(-1, 0, 0, c), at(-1, 0, 1, c), at(1, 0, -1, c), at(0, 2, 0, c), at(0, -2, 0, c)]
    for peer in peers:
        pl.semaphore_signal(barrier, inc=1, device_id=peer, device_id_type=MESH)

    in_copies = [
        pltpu.make_async_copy(routes, rts, l_in.at[0]),
        pltpu.make_async_copy(gates, gts, l_in.at[1]),
        pltpu.make_async_copy(saved, sv, l_in.at[2]),
    ]
    for cp in in_copies:
        cp.start()
    w_copies = [
        pltpu.make_async_copy(w_down.at[:, pl.ds(k * CW, CW)], wv.at[pl.ds(k * width, width)], l_w)
        for k in range(nc)
    ]
    pl.semaphore_wait(barrier, len(peers))

    def send(src, dst, rsem, dev, k):
        pltpu.make_async_remote_copy(
            src_ref=src, dst_ref=dst, send_sem=s_tok.at[k], recv_sem=rsem,
            device_id=dev, device_id_type=MESH,
        ).start()

    def arrived(ref, rsem):
        pltpu.make_async_remote_copy(
            src_ref=ref, dst_ref=ref, send_sem=s_tok.at[0], recv_sem=rsem,
            device_id=at(0, 1, 0, c), device_id_type=MESH,
        ).wait_recv()

    def shard(k, b, dy):
        j = (dy + 2) % NY
        rows = pl.multiple_of((c * 2 + b) * half + (j % (NY // 2)) * toks, toks)
        return tok.at[k, j // (NY // 2), pl.ds(rows, toks), :]

    def far(b, up):
        return 4 if (b == 0) == up else 3

    def y_send(k, b, up, d):
        step = 1 if up else -1
        send(shard(k, b, -step * d), shard(k, b, -step * (d + 1)), r_y.at[k, b * 4 + d], at(0, step, 0, c), k)

    def y_arrived(k, b, d):
        arrived(tok.at[k, 0, pl.ds(0, (2 if d < 4 else 1) * toks), :], r_y.at[k, b * 4 + d - 1])

    def first(k, b):
        arrived(shard(k, b, 0), (r_z, r_x)[b].at[k])
        y_send(k, b, True, 0)
        y_send(k, b, False, 0)

    def hop(k, b, d):
        y_arrived(k, b, d)
        for up in (True, False):
            if d < far(b, up):
                y_send(k, b, up, d)

    def exchange(k, b, p):
        if p == 1:
            y_arrived(k, b, 4)
        ref = tok.at[k, p, pl.ds(pl.multiple_of((c * 2 + b) * half, half), half), :]
        send(ref, ref, r_d.at[k, p], at(0, 0, 0, 1 - c), k)

    def routing(step):
        def tile(dy):
            return meta.at[c * 2 * NY + (y + dy + NY) % NY]

        mine, before = [meta.at[pl.ds(pl.multiple_of((c * 2 + b) * NY, NY), NY)] for b in range(2)]
        if step == 1:
            for dy in (1, -1):
                send(tile(0), tile(0), r_m.at[0], at(0, dy, 0, c), nc)
        elif step == 2:
            arrived(meta.at[pl.ds(0, 2)], r_m.at[0])
            for dy, moved in ((3, (-1, 0, 1)), (-3, (-1, 0))):
                for j in moved:
                    send(tile(j), tile(j), r_m.at[1], at(0, dy, 0, c), nc)
        elif step == 3:
            arrived(meta.at[pl.ds(0, 5)], r_m.at[1])
            send(mine, before, r_m.at[2], at(0, 0, 1, c), nc)
            send(mine, mine, r_m.at[3], at(0, 0, 0, 1 - c), nc)
        else:
            arrived(before, r_m.at[2])
            send(before, before, r_m.at[3], at(0, 0, 0, 1 - c), nc)

    def build_tables():
        arrived(meta.at[pl.ds(0, 2 * NY)], r_m.at[3])
        lane = lax.broadcasted_iota(I32, (8, 128), 1)
        group = lane // toks
        tables = []
        for cs in range(NCORE):
            for b in range(2):
                named = jnp.zeros((8, 128), F32)
                gate = jnp.zeros((8, 128), F32)
                for j in range(NY):
                    m = meta[(cs * 2 + b) * NY + (y + j - 2 + NY) % NY]
                    r = m if j == 0 else pltpu.roll(m, toks * j, 1)
                    shift = (toks * j - toks) % 128
                    g = m if shift == 0 else pltpu.roll(m, shift, 1)
                    named = jnp.where(group == j, r, named)
                    gate = jnp.where(group == j, g, gate)
                for xt in (x, (x - 1 + NX) % NX if b == 0 else (x + 1) % NX):
                    expert = ((y * NX + xt) * NCORE + c).astype(F32)
                    tables.append(jnp.sum(jnp.where(named == expert, gate, 0.0), axis=0, keepdims=True))
        assign = jnp.concatenate(tables, axis=0)
        live = jnp.where(assign > 0.0, 1.0, 0.0).astype(BF)
        from_ = lax.broadcasted_iota(I32, (128, 128), 0)
        to = lax.broadcasted_iota(I32, (128, 128), 1)
        tri = jnp.where((from_ // toks == to // toks) & (from_ < to), 1.0, 0.0).astype(BF)
        before = jnp.dot(live, tri, preferred_element_type=F32)
        before = jnp.where(assign > 0.0, before, -1.0)
        turned = [(assign, before), (pltpu.roll(assign, half, 1), pltpu.roll(before, half, 1))]
        ri = lax.broadcasted_iota(I32, (m16, 128), 0)
        li = lax.broadcasted_iota(I32, (m16, 128), 1)
        same = (ri // MOST) == (li % half) // toks
        place = (ri % MOST).astype(F32)
        for p in range(2):
            for cs in range(NCORE):
                for b in range(2):
                    gates_, places_ = turned[0 if b == p else 1]
                    here = same & (li // half == b)
                    for t in range(2):
                        i = (cs * 2 + b) * 2 + t
                        r0 = (t * 4 + b * 2 + cs) * m16
                        hit = here & (jnp.broadcast_to(places_[i : i + 1], ri.shape) == place)
                        wt = jnp.where(hit, jnp.broadcast_to(gates_[i : i + 1], ri.shape), 0.0)
                        rows = slice(r0, r0 + m16)
                        pick[p, rows, cs * 128 : (cs + 1) * 128] = jnp.where(hit, 1.0, 0.0).astype(BF)
                        pick[p, rows, (1 - cs) * 128 : (2 - cs) * 128] = jnp.zeros((m16, 128), BF)
                        weight[p, rows, :] = jnp.broadcast_to(jnp.sum(wt, axis=1, keepdims=True), (m16, 128))

    def build_perm():
        slot = lax.broadcasted_iota(I32, (256, 256), 0)
        place = lax.broadcasted_iota(I32, (256, 256), 1)
        ys, xs, cs, p = slot // 32, (slot // 8) % NX, (slot // 4) % NCORE, slot % MOST
        dx = (xs - x + NX) % NX
        rel = jnp.where(dx == 0, 0, jnp.where(dx == 3, 1, jnp.where(dx == 1, 2, 3)))
        j = (ys - y + 2 + NY) % NY
        spot = (j // 4) * 128 + rel * 32 + cs * 16 + (j % 4) * MOST + p
        perm[...] = jnp.where(place == spot, 1.0, 0.0).astype(BF)

    def factors(q):
        m = sv.shape[0] // 4
        sl = slice(q * m, (q + 1) * m)
        pre_gate = sv[sl, :width].astype(F32)
        pre_up = sv[sl, width:].astype(F32)
        sig = jax.nn.sigmoid(pre_gate)
        ufac[sl, :] = pre_gate * sig
        gfac[sl, :] = pre_up * sig * (1.0 + pre_gate * (1.0 - sig))

    def select(k, p):
        arrived(tok.at[k, p, pl.ds(0, 2 * half), :], r_d.at[k, p])
        res = jnp.dot(pick[p], tok[k, p], preferred_element_type=F32)
        wt = weight[p]
        rows = jnp.concatenate([res[:, i * 128 : (i + 1) * 128] * wt for i in range(CW // 128)], axis=1).astype(BF)
        snd[k, p, 0] = rows[2 * n : 3 * n]
        snd[k, p, 1] = rows[3 * n : 4 * n]
        row[k, p, 0] = rows[0:n]
        row[k, p, 1] = rows[n : 2 * n]
        send(snd.at[k, p, 0], row.at[k, p, 2], r_r.at[k], at(0, 0, -1, c), k)
        send(snd.at[k, p, 1], row.at[k, p, 3], r_r.at[k], at(0, 0, 1, c), k)

    def main(k):
        arrived(wv.at[pl.ds(0, 4 * n)], r_r.at[k])
        if k == 0:
            pltpu.make_async_copy(wv, wv, l_w).wait()
        lhs = jnp.dot(perm[...], row[k].reshape(256, CW), preferred_element_type=F32).astype(BF)
        for i in range(4):
            cols = slice(i * ncols, (i + 1) * ncols)
            wk = wv[k * width + i * ncols : k * width + (i + 1) * ncols, :]
            part = lax.dot_general(lhs, wk, (((1,), (1,)), ((), ())), preferred_element_type=F32)
            if k > 0:
                part = acc[:, cols] + part
            if k < nc - 1:
                acc[:, cols] = part
            else:
                out[:, cols] = (part * gfac[:, cols]).astype(BF)
                out[:, width + i * ncols : width + (i + 1) * ncols] = (part * ufac[:, cols]).astype(BF)

    for k in range(nc):
        part = grad.at[:, pl.ds(k * CW, CW)]
        send(part, shard(k, 0, 0), r_z.at[k], at(-1, 0, 0, c), k)
        send(part, shard(k, 1, 0), r_x.at[k], at(-1, 0, 1, c), k)
    for cp in w_copies:
        cp.start()
    in_copies[0].wait()
    in_copies[1].wait()
    own = (c * 2) * NY + y
    meta[own, :, 0:toks] = rts[...].astype(F32)
    meta[own, :, toks : 2 * toks] = gts[...]
    routing(1)
    build_perm()
    in_copies[2].wait()
    for q in range(4):
        factors(q)

    for kind, k, b, d in ORDER:
        with jax.named_scope(f"{'fhesmq'[kind]}{b}{d}_{k}"):
            if kind == 0:
                first(k, b)
            elif kind == 1:
                hop(k, b, d)
            elif kind == 2:
                exchange(k, b, d)
            elif kind == 3:
                build_tables() if k == nc else select(k, d)
            elif kind == 4:
                main(k)
            else:
                routing(d)

    for k in range(nc):
        ref = wv.at[pl.ds(0, 16 * toks + 4 * half + 4 * n)]
        pltpu.make_async_copy(ref, ref, s_tok.at[k]).wait()
    ref = meta.at[pl.ds(0, 15 + 2 * NY)]
    pltpu.make_async_copy(ref, ref, s_tok.at[nc]).wait()


def per_device(sections, next_grad, routes, gates, saved, w_down):
    toks, d = next_grad.shape[1:]
    slots, width2 = saved.shape[2:]
    width = width2 // 2
    nc = d // CW
    dma = pltpu.SemaphoreType.DMA
    args = (next_grad[0], routes[0].T, gates[0].T, saved[0, 0], w_down[0])
    res = pl.pallas_call(
        functools.partial(kernel, sections, nc),
        out_shape=jax.ShapeDtypeStruct((slots, width2), BF),
        in_specs=[pl.BlockSpec(memory_space=pltpu.HBM)] * 5,
        out_specs=pl.BlockSpec(memory_space=pltpu.VMEM),
        scratch_shapes=[
            pltpu.VMEM((nc, 2, NCORE * NY * toks, CW), BF),
            pltpu.VMEM((nc, 2, 4, NY * MOST, CW), BF),
            pltpu.VMEM((nc, 2, 2, NY * MOST, CW), BF),
            pltpu.VMEM((nc * width, CW), BF),
            pltpu.VMEM((slots, width2), BF),
            pltpu.VMEM((slots, width), F32),
            pltpu.VMEM((slots, width), F32),
            pltpu.VMEM((slots, width), F32),
            pltpu.VMEM(routes.shape[:0:-1], I32),
            pltpu.VMEM(gates.shape[:0:-1], F32),
            pltpu.VMEM((NCORE * 2 * NY, 8, 128), F32),
            pltpu.VMEM((2, 128, 256), BF),
            pltpu.VMEM((2, 128, 128), F32),
            pltpu.VMEM((256, 256), BF),
            dma((nc, 8)),
            dma((nc,)),
            dma((nc,)),
            dma((nc, 2)),
            dma((nc,)),
            dma((4,)),
            dma((nc + 1,)),
            dma((3,)),
            dma,
        ],
        compiler_params=pltpu.CompilerParams(collective_id=0, has_side_effects=True, vmem_limit_bytes=40 << 20),
    )(*[pltpu.with_memory_space_constraint(v, pltpu.HBM) for v in args])
    return res[None, None]


def solution(mesh):
    return jax.shard_map(
        functools.partial(per_device, mesh.shape["section"]),
        mesh=mesh,
        in_specs=(
            P("section", "expert", None),
            P("section", "expert", None),
            P("section", "expert", None),
            P("section", "expert", None, None),
            P("expert", None, None),
        ),
        out_specs=P("section", "expert", None, None),
        check_vma=False,
    )
```
